32 devices in a mesh: grp: 2 (over y), ctx: 4 (over z), kvh: 2 (over x), sub: 2 (over core).
Axes of the slice: x: 2, y: 2, z: 4, core: 2. Of those that a mesh axis runs over, the one named last changes fastest.
Arguments:
- queries: bfloat16 [1024, 8, 8, 128], P(('grp', 'ctx'), 'kvh', 'sub'), parts along dimension 0
- new_keys: bfloat16 [1024, 8, 128], P(('grp', 'ctx'), 'kvh'), parts along dimension 0
- new_values: bfloat16 [1024, 8, 128], P(('grp', 'ctx'), 'kvh'), parts along dimension 0, may hold values from -6 to 6
- cache_keys: bfloat16 [16384, 8, 128], P(('grp', 'ctx'), 'kvh'), parts along dimension 0, may hold values from -16 to 16
- cache_values: bfloat16 [16384, 8, 128], P(('grp', 'ctx'), 'kvh'), parts along dimension 0, may hold values from -6 to 6
- vertical_pool: int32 [16], P(('grp', 'ctx')), parts along dimension 0, may hold values from 0 to 15, as said below
- vertical_lists: int32 [8, 6], P(('grp', 'ctx')), parts along dimension 0, may hold values from 0 to 7, as said below
- slash_lists: int32 [8, 2], P(('grp', 'ctx')), parts along dimension 0, may hold values from 0 to 1, as said below
- list_counts: int32 [8, 2], P(('grp', 'ctx')), parts along dimension 0, may hold values from 1 to 6, as said below
Outputs:
- attention: bfloat16 [1024, 8, 8, 128], P(('grp', 'ctx'), 'kvh', 'sub'), parts along dimension 0
The draws below stay inside these ranges and needn't reach their ends.
There are 2 independent parts, one for each index of `grp`. The reference program is written for one: setup_inputs(seed, part) draws one part's arguments, and reference() takes and returns one part's arrays. A program takes and returns all parts, laid end to end along the dimension named above; each array names one. Nothing has to cross between parts.
Inputs may be any that keep to these rules, and one draw needn't show every extreme that they name: `vertical_pool`: the 2 entries of one index of ctx are distinct. `vertical_lists`: in row b the first list_counts[b, 0] entries are distinct; later entries are never read. `slash_lists`: row b begins with 0; its first list_counts[b, 1] entries are distinct and none exceeds b or 1 plus b modulo 1; later entries are never read. `list_counts`: column 0 lies between 1 and 6, column 1 between 1 and 2, each reached in every draw.
All inputs are finite; a program needn't handle non-finite values.
Results may differ from the reference program's by a relative error of at most 0.014.
Values may be sent and summed in bfloat16 or wider, within the bound.
No kernel may reach another device: no remote copies, remote signals or barrier semaphores. Data moves between devices by JAX's collectives and lax.ppermute only.
A program may use at most 64 MiB of HBM per device.

```python
import jax
import jax.numpy as jnp
from jax import lax

KVH = 8
HD = 128
GROUPS = 8
BLK = 128
P_DEV = 2048
VD = 2
QB_DEV = 1
NQB = 4
QTOT = 512
PREFIX = 8192
POOL = 8
VMAX = 6
SMAX = 2


def draw_queries(key, part):
    drawn = jnp.clip(jax.random.normal(key, (QTOT, KVH, GROUPS, HD), jnp.float32), -8.0, 8.0)
    return drawn.astype(jnp.bfloat16)


def draw_new_keys(key, part):
    drawn = jnp.clip(2.5 * jax.random.normal(key, (QTOT, KVH, HD), jnp.float32), -16.0, 16.0)
    return drawn.astype(jnp.bfloat16)


def draw_vertical_pool(key, part):
    blocks_dev = P_DEV // BLK
    owners = POOL // VD
    subkeys = jax.random.split(jax.random.fold_in(key, 11), owners)
    rows = jax.vmap(lambda subkey: jax.random.permutation(subkey, blocks_dev)[:VD])(subkeys).astype(jnp.int32)
    chosen = jax.random.randint(jax.random.fold_in(key, 12), (), 0, owners)
    position = jnp.arange(VD, dtype=jnp.int32)
    ends = jnp.where(position == VD - 1, blocks_dev - 1, position).astype(jnp.int32)
    rows = jnp.where(jnp.arange(owners)[:, None] == chosen, ends[None, :], rows)
    return rows.reshape(POOL).astype(jnp.int32)


def list_tables(key):
    drawn = jax.random.fold_in(key, 21)
    subkeys = jax.random.split(drawn, 4)
    blocks = jnp.arange(NQB, dtype=jnp.int32)
    jitter = jax.random.randint(subkeys[0], (NQB,), 0, VMAX // 8 + 1)
    jitter = jnp.where(blocks == NQB - 1, 0, jitter)
    vertical_count = jnp.maximum(VMAX * (blocks + 1) // NQB - jitter, 1)
    vertical = jax.vmap(lambda subkey: jax.random.permutation(subkey, POOL)[:VMAX])(jax.random.split(subkeys[1], NQB))
    local_index = blocks % QB_DEV
    reach_limit = jnp.minimum(blocks, QB_DEV + local_index)
    slash_count = jax.random.randint(subkeys[2], (NQB,), 1, reach_limit + 2)
    slash_count = jnp.where(blocks == NQB - 1, reach_limit + 1, slash_count)
    candidates = jax.vmap(lambda subkey: jax.random.permutation(subkey, SMAX - 1) + 1)(jax.random.split(subkeys[3], NQB))
    position = jnp.arange(SMAX - 1, dtype=jnp.int32)
    order_key = (candidates > reach_limit[:, None]).astype(jnp.int32) * SMAX + position[None, :]
    ordering = jnp.argsort(order_key, axis=1)
    ordered = jnp.take_along_axis(candidates, ordering, axis=1)
    slash_rows = jnp.concatenate([jnp.zeros((NQB, 1), jnp.int32), ordered.astype(jnp.int32)], axis=1)
    counts = jnp.stack([vertical_count, slash_count], axis=1)
    return (vertical.astype(jnp.int32), slash_rows.astype(jnp.int32), counts.astype(jnp.int32))


def draw_vertical_lists(key, part):
    return list_tables(key)[0]


def draw_slash_lists(key, part):
    return list_tables(key)[1]


def draw_list_counts(key, part):
    return list_tables(key)[2]


def levels(own_key, extent, pieces, least, high):
    factor_of = 1.0
    for axis_at, parts in pieces:
        heights = jax.random.uniform(jax.random.fold_in(jax.random.fold_in(own_key, 6), axis_at), (parts,), jnp.float32, least / len(pieces), high / len(pieces))
        factor_of = factor_of * jnp.repeat(jnp.exp(heights), extent[axis_at] // parts).reshape((-1,) + (1,) * (len(extent) - 1 - axis_at))
    return factor_of


def bell_draw(rng, dims, width, bound, pieces=(), kind=jnp.bfloat16):
    values = jax.random.normal(rng, dims, jnp.float32) * width
    if len(pieces) > 0:
        values = levels(rng, dims, pieces, -0.22, 0.18) * values
    return jnp.clip(values, min=-bound, max=bound).astype(kind)


def setup_inputs(seed: int = 0, part: int = 0) -> dict:
    arg_keys = jax.random.split(jax.random.key(seed), 10)
    own_keys = jax.random.split(jax.random.fold_in(arg_keys[9], part), 10)
    queries = draw_queries(jax.random.fold_in(jax.random.fold_in(arg_keys[9], part), 71), part)
    new_keys = draw_new_keys(jax.random.fold_in(jax.random.fold_in(arg_keys[9], part), 71), part)
    new_values = bell_draw(own_keys[2], (QTOT, KVH, HD), 1.0, 6.0, ((0, 4), (1, 2)))
    cache_keys = bell_draw(own_keys[3], (PREFIX, KVH, HD), 2.5, 16.0, ((0, 4), (1, 2)))
    cache_values = bell_draw(own_keys[4], (PREFIX, KVH, HD), 1.0, 6.0, ((0, 4), (1, 2)))
    vertical_pool = draw_vertical_pool(jax.random.fold_in(jax.random.fold_in(arg_keys[9], part), 71), part)
    vertical_lists = draw_vertical_lists(jax.random.fold_in(jax.random.fold_in(arg_keys[9], part), 71), part)
    slash_lists = draw_slash_lists(jax.random.fold_in(jax.random.fold_in(arg_keys[9], part), 71), part)
    list_counts = draw_list_counts(jax.random.fold_in(jax.random.fold_in(arg_keys[9], part), 71), part)
    return dict(queries=queries, new_keys=new_keys, new_values=new_values, cache_keys=cache_keys, cache_values=cache_values, vertical_pool=vertical_pool, vertical_lists=vertical_lists, slash_lists=slash_lists, list_counts=list_counts)


def block_update(carry_state, query_block, block_keys, block_values, visible):
    row_peak, row_total, numerator = carry_state
    score_scale = query_block.shape[-1] ** -0.5
    scores = jnp.einsum("rkgd,ckd->rkgc", query_block.astype(jnp.float32), block_keys.astype(jnp.float32)) * score_scale
    scores = jnp.where(visible, scores, -jnp.inf)
    new_peak = jnp.maximum(row_peak, jnp.max(scores, axis=3))
    factor = jnp.exp(row_peak - new_peak)
    weights = jnp.exp(scores - new_peak[..., None])
    row_total = row_total * factor + jnp.sum(weights, axis=3)
    rounded = lax.optimization_barrier(weights.astype(jnp.bfloat16)).astype(jnp.float32)
    numerator = numerator * factor[..., None] + jnp.einsum("rkgc,ckd->rkgd", rounded, block_values.astype(jnp.float32))
    return new_peak, row_total, numerator


def reference(queries, new_keys, new_values, cache_keys, cache_values, vertical_pool, vertical_lists, slash_lists, list_counts):
    blocks_dev = P_DEV // BLK
    owners = jnp.arange(POOL, dtype=jnp.int32) // VD
    pool_sources = (owners * blocks_dev + vertical_pool).astype(jnp.int32)
    cached_keys = cache_keys.reshape(PREFIX // BLK, BLK, KVH, HD)
    cached_values = cache_values.reshape(PREFIX // BLK, BLK, KVH, HD)
    fresh_keys = new_keys.reshape(NQB, BLK, KVH, HD)
    fresh_values = new_values.reshape(NQB, BLK, KVH, HD)
    query_grid = queries.reshape(NQB, BLK, KVH, GROUPS, HD)
    row_ids = lax.broadcasted_iota(jnp.int32, (BLK, 1, 1, BLK), 0)
    col_ids = lax.broadcasted_iota(jnp.int32, (BLK, 1, 1, BLK), 3)
    causal = col_ids <= row_ids

    def one_block(block_index):
        query_block = query_grid[block_index]
        blank_state = (jnp.full((BLK, KVH, GROUPS), -jnp.inf, jnp.float32),
                       jnp.zeros((BLK, KVH, GROUPS), jnp.float32),
                       jnp.zeros((BLK, KVH, GROUPS, HD), jnp.float32))

        def vertical_step(step_index, carry_state):
            source = pool_sources[vertical_lists[block_index, step_index]]
            return block_update(carry_state, query_block, cached_keys[source], cached_values[source], True)

        carry_state = lax.fori_loop(0, list_counts[block_index, 0], vertical_step, blank_state)

        def slash_step(step_index, carry_state):
            offset = slash_lists[block_index, step_index]
            target = block_index - offset
            return block_update(carry_state, query_block, fresh_keys[target], fresh_values[target], causal | (offset > 0))

        carry_state = lax.fori_loop(0, list_counts[block_index, 1], slash_step, carry_state)
        return (carry_state[2] / carry_state[1][..., None]).astype(jnp.bfloat16)

    result = lax.map(one_block, jnp.arange(NQB, dtype=jnp.int32))
    return result.reshape(QTOT, KVH, GROUPS, HD)
```

```python
import functools
import math

import jax
import jax.numpy as jnp
from jax import lax
from jax.experimental import pallas as pl
from jax.experimental.pallas import tpu as pltpu
from jax.sharding import PartitionSpec as P

BLK = 128

VMEM = pltpu.VMEM
SMEM = pltpu.SMEM


def vmem_spec():
    return pl.BlockSpec(memory_space=VMEM)


def smem_spec():
    return pl.BlockSpec(memory_space=SMEM)


def hbm_spec():
    return pl.BlockSpec(memory_space=pl.ANY)


def split_heads(wide, rows, heads, block):
    return wide[pl.ds(block, rows, stride=heads), :].astype(jnp.bfloat16)


def gather_kernel(heads, per_core, pool, ck, cv, nk, nv, piece, fresh, raw, wide, sems, fresh_sem):
    core = lax.axis_index("sub")
    rows = BLK * heads
    copies = []
    for j in range(per_core):
        block = pool[core * per_core + j]
        for which, cache in enumerate((ck, cv)):
            copy = pltpu.make_async_copy(
                cache.at[block], raw.at[which * per_core + j], sems.at[which * per_core + j]
            )
            copy.start()
            copies.append(copy)

    @pl.when(core == 0)
    def _():
        pltpu.make_async_copy(nk, fresh, fresh_sem).start()

    @pl.when(core != 0)
    def _():
        pltpu.make_async_copy(nv, fresh, fresh_sem).start()

    for j in range(per_core):
        for which in range(2):
            copies[2 * j + which].wait()
            slot = which * per_core + j
            wide[slot] = raw[slot].astype(jnp.float32)
            for h in range(heads):
                piece[which, pl.ds((j * heads + h) * BLK, BLK), :] = split_heads(
                    wide.at[slot], BLK, heads, h
                )
    pltpu.make_async_copy(nk, fresh, fresh_sem).wait()


def gather(pool, ck, cv, nk, nv, heads, per_core):
    dim = ck.shape[-1]
    rows = BLK * heads
    slots = 2 * per_core
    return pl.pallas_call(
        functools.partial(gather_kernel, heads, per_core),
        out_shape=(
            jax.ShapeDtypeStruct((2, per_core * rows, dim), jnp.bfloat16),
            jax.ShapeDtypeStruct(nk.shape, jnp.bfloat16),
        ),
        in_specs=[smem_spec(), hbm_spec(), hbm_spec(), hbm_spec(), hbm_spec()],
        out_specs=(vmem_spec(), vmem_spec()),
        scratch_shapes=[
            VMEM((slots, rows, dim), jnp.bfloat16),
            VMEM((slots, rows, dim), jnp.float32),
            pltpu.SemaphoreType.DMA((slots,)),
            pltpu.SemaphoreType.DMA(()),
        ],
        name="gather",
    )(pool, ck, cv, nk, nv)


class Shape:
    def __init__(self, tokens, heads, groups, dim, vertical, cores):
        self.tokens, self.heads, self.groups, self.dim = tokens, heads, groups, dim
        self.rows = tokens * groups
        self.vertical, self.cores = vertical, cores
        self.per_core = vertical // cores
        self.scale = dim ** (-0.5) * math.log2(math.e)


def listed(entries, count, value):
    found = jnp.int32(0)
    for i in range(entries.shape[1]):
        hit = jnp.logical_and(i < count, entries[0, i] == value)
        found = jnp.maximum(found, hit.astype(jnp.int32))
    return found


def absorb(shape, q, m, acc, h, keys, values, lives, causal=False, first=False):
    dim = shape.dim
    scores = lax.dot_general(
        q[h], keys, (((1,), (1,)), ((), ())), preferred_element_type=jnp.float32
    )
    parts = []
    for i, live in enumerate(lives):
        part = scores[:, i * BLK : (i + 1) * BLK] * shape.scale
        if causal:
            row = lax.broadcasted_iota(jnp.int32, part.shape, 0) & (shape.tokens - 1)
            col = lax.broadcasted_iota(jnp.int32, part.shape, 1)
            part = jnp.where(col <= row, part, -jnp.inf)
        if live is not None:
            part = part + jnp.where(live > 0, 0.0, -jnp.inf)
        parts.append(part)
    highest = parts[0]
    for part in parts[1:]:
        highest = jnp.maximum(highest, part)
    highest = jnp.max(highest, axis=1, keepdims=True)
    if first:
        peak = jnp.broadcast_to(highest, (shape.rows, BLK))
    else:
        old = m[h]
        peak = jnp.maximum(old, highest)
    weights = jnp.concatenate(
        [jnp.exp2(part - peak).astype(jnp.bfloat16) for part in parts], axis=1
    )
    wide_values = jnp.concatenate([values, jnp.ones_like(values)], axis=1)
    added = jnp.dot(weights, wide_values, preferred_element_type=jnp.float32)
    if first:
        acc[h] = added
    else:
        factor = jnp.exp2(old - peak)
        acc[h] = acc[h] * jnp.concatenate([factor, factor], axis=1) + added
    m[h] = peak


def absorb_pieces(shape, vl, counts, q, m, acc, offset, pieces):
    owner = lax.axis_index("ctx") ^ offset
    core = lax.axis_index("sub")
    lives = []
    for away in range(shape.cores):
        source = core ^ away
        for j in range(shape.per_core):
            slot = owner * shape.vertical + source * shape.per_core + j
            lives.append(listed(vl, counts[0, 0], slot))
    any_live = functools.reduce(jnp.maximum, lives)

    @pl.when(any_live > 0)
    def _():
        for h in range(shape.heads):
            spans = [
                (piece, pl.ds((j * shape.heads + h) * BLK, BLK))
                for piece in pieces
                for j in range(shape.per_core)
            ]
            keys = jnp.concatenate([piece[0, span, :] for piece, span in spans], axis=0)
            values = jnp.concatenate([piece[1, span, :] for piece, span in spans], axis=0)
            absorb(shape, q, m, acc, h, keys, values, lives)


def finish(shape, acc, out, wide):
    stride = shape.heads * shape.groups
    for h in range(shape.heads):
        done = acc[h, :, : shape.dim] / acc[h, :, shape.dim :]
        for g in range(shape.groups):
            wide[pl.ds(h * shape.groups + g, shape.tokens, stride=stride), :] = done[
                g * shape.tokens : (g + 1) * shape.tokens
            ]
    out[...] = wide[...].astype(jnp.bfloat16)


def attend_kernel(shape, first, last, offsets, with_fresh, *refs):
    refs = list(refs)
    vl, sl, counts = refs[:3]
    refs = refs[3:]
    if first:
        raw_q, nk, nv = refs[:3]
        refs = refs[3:]
    else:
        q, m_in, acc_in = refs[:3]
        refs = refs[3:]
    if with_fresh:
        fresh = refs[: shape.cores]
        refs = refs[shape.cores :]
    pieces = []
    for _ in offsets:
        pieces.append(refs[: shape.cores])
        refs = refs[shape.cores :]
    if first:
        q, m, acc = refs[:3]
        refs = refs[3:]
    elif not last:
        m, acc = refs[:2]
        refs = refs[2:]
    else:
        out = refs[0]
        m, acc = refs[1:3]
        refs = refs[3:]
    wide_q, wide_kv = refs

    if first:
        stride = shape.heads * shape.groups
        wide_q[...] = raw_q[...].astype(jnp.float32)
        for h in range(shape.heads):
            for g in range(shape.groups):
                q[h, pl.ds(g * shape.tokens, shape.tokens), :] = split_heads(
                    wide_q, shape.tokens, stride, h * shape.groups + g
                )
        wide_kv[0] = nk[...].astype(jnp.float32)
        wide_kv[1] = nv[...].astype(jnp.float32)
        for h in range(shape.heads):
            keys = split_heads(wide_kv.at[0], BLK, shape.heads, h)
            values = split_heads(wide_kv.at[1], BLK, shape.heads, h)
            absorb(shape, q, m, acc, h, keys, values, [None], causal=True, first=True)
    else:
        m[...] = m_in[...]
        acc[...] = acc_in[...]

    if with_fresh:

        @pl.when(listed(sl, counts[0, 1], 1) > 0)
        def _():
            core = lax.axis_index("sub")
            for away in range(shape.cores):
                wide_kv[core ^ away] = fresh[away][...].astype(jnp.float32)
            for h in range(shape.heads):
                keys = split_heads(wide_kv.at[0], BLK, shape.heads, h)
                values = split_heads(wide_kv.at[1], BLK, shape.heads, h)
                absorb(shape, q, m, acc, h, keys, values, [None])

    for offset, arrays in zip(offsets, pieces):
        absorb_pieces(shape, vl, counts, q, m, acc, offset, arrays)

    if last:
        finish(shape, acc, out, wide_q)


def attend(shape, lists, state, offsets, pieces, fresh=(), first=False, last=False, name=None):
    stacked = (shape.heads, shape.rows)
    state_shapes = [
        jax.ShapeDtypeStruct(stacked + (BLK,), jnp.float32),
        jax.ShapeDtypeStruct(stacked + (2 * shape.dim,), jnp.float32),
    ]
    flat = shape.tokens * shape.heads * shape.groups
    scratch = [
        VMEM((flat, shape.dim), jnp.float32),
        VMEM((2, BLK * shape.heads, shape.dim), jnp.float32),
    ]
    aliases = {}
    if first:
        outs = [jax.ShapeDtypeStruct(stacked + (shape.dim,), jnp.bfloat16)] + state_shapes
    elif not last:
        outs = state_shapes
    else:
        outs = [jax.ShapeDtypeStruct((flat, shape.dim), jnp.bfloat16)]
        scratch = [VMEM(s.shape, s.dtype) for s in state_shapes] + scratch
    operands = [*lists, *state, *fresh, *[a for arrays in pieces for a in arrays]]
    return pl.pallas_call(
        functools.partial(attend_kernel, shape, first, last, offsets, bool(fresh)),
        out_shape=outs,
        in_specs=[smem_spec()] * 3 + [vmem_spec()] * (len(operands) - 3),
        out_specs=[vmem_spec()] * len(outs),
        scratch_shapes=scratch,
        input_output_aliases=aliases,
        compiler_params=pltpu.CompilerParams(vmem_limit_bytes=40 << 20),
        name=name,
    )(*operands)


def shards(mesh_shape, queries, nk, nv, ck, cv, pool, vl, sl, counts):
    n, cores = mesh_shape["ctx"], mesh_shape["sub"]
    tokens, heads, groups, dim = queries.shape
    shape = Shape(tokens, heads, groups, dim, pool.shape[0], cores)
    flat_q = queries.reshape(tokens * heads * groups, dim)
    flat_nk = nk.reshape(tokens * heads, dim)
    flat_nv = nv.reshape(tokens * heads, dim)
    blocks = ck.shape[0] // BLK
    flat_ck = ck.reshape(blocks, BLK * heads, dim)
    flat_cv = cv.reshape(blocks, BLK * heads, dim)
    lists = (vl, sl, counts)

    def exchange(x, away):
        return lax.ppermute(x, "ctx", [(i, i ^ away) for i in range(n)])

    def both(x):
        return [x] + [
            lax.ppermute(x, "sub", [(i, i ^ away) for i in range(cores)])
            for away in range(1, cores)
        ]

    own, fresh = gather(pool, flat_ck, flat_cv, flat_nk, flat_nv, heads, shape.per_core)
    held = {0: own}
    order = sorted(range(1, n), key=lambda o: (bin(o).count("1"), -o))
    for offset in order:
        low = offset & -offset
        held[offset] = exchange(held[offset ^ low], low)
    earlier = lax.ppermute(fresh, "ctx", [(i, i + 1) for i in range(n - 1)])

    state = attend(
        shape, lists, (flat_q, flat_nk, flat_nv), [0], [both(held[0])], first=True, name="local"
    )
    q = state[0]
    state = attend(
        shape, lists, state, order[:-1], [both(held[o]) for o in order[:-1]],
        fresh=both(earlier), name="middle",
    )
    (out,) = attend(
        shape, lists, (q, *state), order[-1:], [both(held[o]) for o in order[-1:]],
        last=True, name="tail",
    )
    return out.reshape(queries.shape)


def solution(mesh):
    mesh_shape = dict(mesh.shape)
    n, cores = mesh_shape["ctx"], mesh_shape["sub"]
    if n & (n - 1) or cores != 2:
        raise ValueError("unsupported mesh")
    split = ("grp", "ctx")
    in_specs = (
        P(split, "kvh", "sub", None),
        P(split, "kvh", None),
        P(split, "kvh", None),
        P(split, "kvh", None),
        P(split, "kvh", None),
        P(split),
        P(split, None),
        P(split, None),
        P(split, None),
    )
    out_specs = P(split, "kvh", "sub", None)
    return jax.shard_map(
        functools.partial(shards, mesh_shape),
        mesh=mesh,
        in_specs=in_specs,
        out_specs=out_specs,
        check_vma=False,
    )
```

```python
import functools
import math

import jax
import jax.numpy as jnp
from jax import lax
from jax.experimental import pallas as pl
from jax.experimental.pallas import tpu as pltpu
from jax.sharding import PartitionSpec as P


BLK = 128

VMEM = pltpu.VMEM
SMEM = pltpu.SMEM


def vmem_spec():
    return pl.BlockSpec(memory_space=VMEM)


def smem_spec():
    return pl.BlockSpec(memory_space=SMEM)


def hbm_spec():
    return pl.BlockSpec(memory_space=pl.ANY)


def split_heads(wide, rows, heads, block):
    return wide[pl.ds(block, rows, stride=heads), :].astype(jnp.bfloat16)


def gather_kernel(heads, per_core, pool, ck, cv, nk, nv, piece, fresh, raw, wide, sems, fresh_sem):
    core = lax.axis_index("sub")
    copies = []
    for j in range(per_core):
        block = pool[core * per_core + j]
        for which, cache in enumerate((ck, cv)):
            copy = pltpu.make_async_copy(
                cache.at[block], raw.at[which * per_core + j], sems.at[which * per_core + j]
            )
            copy.start()
            copies.append(copy)

    @pl.when(core == 0)
    def _():
        pltpu.make_async_copy(nk, fresh, fresh_sem).start()

    @pl.when(core != 0)
    def _():
        pltpu.make_async_copy(nv, fresh, fresh_sem).start()

    for j in range(per_core):
        for which in range(2):
            copies[2 * j + which].wait()
            slot = which * per_core + j
            wide[slot] = raw[slot].astype(jnp.float32)
            for h in range(heads):
                piece[which, pl.ds((j * heads + h) * BLK, BLK), :] = split_heads(
                    wide.at[slot], BLK, heads, h
                )
    pltpu.make_async_copy(nk, fresh, fresh_sem).wait()


def gather(pool, ck, cv, nk, nv, heads, per_core):
    dim = ck.shape[-1]
    rows = BLK * heads
    slots = 2 * per_core
    return pl.pallas_call(
        functools.partial(gather_kernel, heads, per_core),
        out_shape=(
            jax.ShapeDtypeStruct((2, per_core * rows, dim), jnp.bfloat16),
            jax.ShapeDtypeStruct(nk.shape, jnp.bfloat16),
        ),
        in_specs=[smem_spec(), hbm_spec(), hbm_spec(), hbm_spec(), hbm_spec()],
        out_specs=(vmem_spec(), vmem_spec()),
        scratch_shapes=[
            VMEM((slots, rows, dim), jnp.bfloat16),
            VMEM((slots, rows, dim), jnp.float32),
            pltpu.SemaphoreType.DMA((slots,)),
            pltpu.SemaphoreType.DMA(()),
        ],
        name="gather",
    )(pool, ck, cv, nk, nv)


class Shape:
    def __init__(self, tokens, heads, groups, dim, vertical, cores):
        self.tokens, self.heads, self.groups, self.dim = tokens, heads, groups, dim
        self.rows = tokens * groups
        self.vertical, self.cores = vertical, cores
        self.per_core = vertical // cores
        self.scale = dim ** (-0.5) * math.log2(math.e)


def listed(entries, count, value):
    found = jnp.int32(0)
    for i in range(entries.shape[1]):
        hit = jnp.logical_and(i < count, entries[0, i] == value)
        found = jnp.maximum(found, hit.astype(jnp.int32))
    return found


def absorb(shape, q, m, acc, h, keys, values, lives, causal=False, first=False, keep=True):
    scores = lax.dot_general(
        q[h], keys, (((1,), (1,)), ((), ())), preferred_element_type=jnp.float32
    )
    parts = []
    for i, live in enumerate(lives):
        part = scores[:, i * BLK : (i + 1) * BLK] * shape.scale
        if causal:
            row = lax.broadcasted_iota(jnp.int32, part.shape, 0) & (shape.tokens - 1)
            col = lax.broadcasted_iota(jnp.int32, part.shape, 1)
            part = jnp.where(col <= row, part, -jnp.inf)
        if live is not None:
            part = part + jnp.where(live > 0, 0.0, -jnp.inf)
        parts.append(part)
    highest = parts[0]
    for part in parts[1:]:
        highest = jnp.maximum(highest, part)
    highest = jnp.max(highest, axis=1, keepdims=True)
    if first:
        peak = jnp.broadcast_to(highest, (shape.rows, BLK))
    else:
        old = m[h]
        peak = jnp.maximum(old, highest)
    weights = jnp.concatenate(
        [jnp.exp2(part - peak).astype(jnp.bfloat16) for part in parts], axis=1
    )
    wide_values = jnp.concatenate([values, jnp.ones_like(values)], axis=1)
    total = jnp.dot(weights, wide_values, preferred_element_type=jnp.float32)
    if not first:
        factor = jnp.exp2(old - peak)
        total = acc[h] * jnp.concatenate([factor, factor], axis=1) + total
    if keep:
        acc[h] = total
        m[h] = peak
    return total


def piece_lives(shape, vl, counts, offset):
    owner = lax.axis_index("ctx") ^ offset
    core = lax.axis_index("sub")
    lives = []
    for away in range(shape.cores):
        source = core ^ away
        for j in range(shape.per_core):
            slot = owner * shape.vertical + source * shape.per_core + j
            lives.append(listed(vl, counts[0, 0], slot))
    return lives, functools.reduce(jnp.maximum, lives)


def piece_head(shape, pieces, which, h):
    spans = [pl.ds((j * shape.heads + h) * BLK, BLK) for j in range(shape.per_core)]
    return jnp.concatenate([piece[which, span, :] for piece in pieces for span in spans], axis=0)


def store_head(shape, wide, h, total):
    stride = shape.heads * shape.groups
    done = total[:, : shape.dim] / total[:, shape.dim :]
    for g in range(shape.groups):
        wide[pl.ds(h * shape.groups + g, shape.tokens, stride=stride), :] = done[
            g * shape.tokens : (g + 1) * shape.tokens
        ]


def attend_kernel(shape, first, last, offsets, with_fresh, *refs):
    refs = list(refs)

    def take(count):
        taken = refs[:count]
        del refs[:count]
        return taken

    vl, sl, counts = take(3)
    if first:
        raw_q, nk, nv = take(3)
    else:
        q, m, acc = take(3)
    fresh = take(shape.cores) if with_fresh else []
    pieces = [take(shape.cores) for _ in offsets]
    if first:
        q, m, acc = take(3)
    elif not last:
        m, acc = take(2)
    else:
        (out,) = take(1)
    wide_q, wide_kv = refs

    if first:
        stride = shape.heads * shape.groups
        wide_q[...] = raw_q[...].astype(jnp.float32)
        for h in range(shape.heads):
            for g in range(shape.groups):
                q[h, pl.ds(g * shape.tokens, shape.tokens), :] = split_heads(
                    wide_q, shape.tokens, stride, h * shape.groups + g
                )
        wide_kv[0] = nk[...].astype(jnp.float32)
        wide_kv[1] = nv[...].astype(jnp.float32)
        for h in range(shape.heads):
            keys = split_heads(wide_kv.at[0], BLK, shape.heads, h)
            values = split_heads(wide_kv.at[1], BLK, shape.heads, h)
            absorb(shape, q, m, acc, h, keys, values, [None], causal=True, first=True)

    if with_fresh:

        @pl.when(listed(sl, counts[0, 1], 1) > 0)
        def _():
            core = lax.axis_index("sub")
            for away in range(shape.cores):
                wide_kv[core ^ away] = fresh[away][...].astype(jnp.float32)
            for h in range(shape.heads):
                keys = split_heads(wide_kv.at[0], BLK, shape.heads, h)
                values = split_heads(wide_kv.at[1], BLK, shape.heads, h)
                absorb(shape, q, m, acc, h, keys, values, [None])

    for offset, arrays in zip(offsets, pieces):
        lives, any_live = piece_lives(shape, vl, counts, offset)

        @pl.when(any_live > 0)
        def _():
            for h in range(shape.heads):
                keys = piece_head(shape, arrays, 0, h)
                values = piece_head(shape, arrays, 1, h)
                total = absorb(shape, q, m, acc, h, keys, values, lives, keep=not last)
                if last:
                    store_head(shape, wide_q, h, total)

        if last:

            @pl.when(any_live == 0)
            def _():
                for h in range(shape.heads):
                    store_head(shape, wide_q, h, acc[h])

    if last:
        out[...] = wide_q[...].astype(jnp.bfloat16)


def attend(shape, lists, state, offsets, pieces, fresh=(), first=False, last=False):
    stacked = (shape.heads, shape.rows)
    state_shapes = [
        jax.ShapeDtypeStruct(stacked + (BLK,), jnp.float32),
        jax.ShapeDtypeStruct(stacked + (2 * shape.dim,), jnp.float32),
    ]
    flat = shape.tokens * shape.heads * shape.groups
    scratch = [
        VMEM((flat, shape.dim), jnp.float32),
        VMEM((2, BLK * shape.heads, shape.dim), jnp.float32),
    ]
    aliases = {}
    if first:
        outs = [jax.ShapeDtypeStruct(stacked + (shape.dim,), jnp.bfloat16)] + state_shapes
    elif not last:
        outs = state_shapes
        aliases = {4: 0, 5: 1}
    else:
        outs = [jax.ShapeDtypeStruct((flat, shape.dim), jnp.bfloat16)]
    operands = [*lists, *state, *fresh, *[a for arrays in pieces for a in arrays]]
    return pl.pallas_call(
        functools.partial(attend_kernel, shape, first, last, offsets, bool(fresh)),
        out_shape=outs,
        in_specs=[smem_spec()] * 3 + [vmem_spec()] * (len(operands) - 3),
        out_specs=[vmem_spec()] * len(outs),
        scratch_shapes=scratch,
        input_output_aliases=aliases,
        compiler_params=pltpu.CompilerParams(vmem_limit_bytes=40 << 20),
    )(*operands)


def shards(mesh_shape, queries, nk, nv, ck, cv, pool, vl, sl, counts):
    n, cores = mesh_shape["ctx"], mesh_shape["sub"]
    tokens, heads, groups, dim = queries.shape
    shape = Shape(tokens, heads, groups, dim, pool.shape[0], cores)
    flat_q = queries.reshape(tokens * heads * groups, dim)
    flat_nk = nk.reshape(tokens * heads, dim)
    flat_nv = nv.reshape(tokens * heads, dim)
    blocks = ck.shape[0] // BLK
    flat_ck = ck.reshape(blocks, BLK * heads, dim)
    flat_cv = cv.reshape(blocks, BLK * heads, dim)
    lists = (vl, sl, counts)

    def exchange(x, away):
        return lax.ppermute(x, "ctx", [(i, i ^ away) for i in range(n)])

    def both(x):
        return [x] + [
            lax.ppermute(x, "sub", [(i, i ^ away) for i in range(cores)])
            for away in range(1, cores)
        ]

    own, fresh = gather(pool, flat_ck, flat_cv, flat_nk, flat_nv, heads, shape.per_core)
    order = sorted(range(1, n), key=lambda o: (bin(o).count("1"), -o))
    held = {0: own}
    for offset in order:
        low = offset & -offset
        held[offset] = exchange(held[offset ^ low], low)
    earlier = lax.ppermute(fresh, "ctx", [(i, i + 1) for i in range(n - 1)])
    pieces = {o: both(held[o]) for o in held}
    fresh = both(earlier)
    state = attend(
        shape, lists, (flat_q, flat_nk, flat_nv), [0], [pieces[0]],
        first=True,
    )
    q = state[0]
    state = attend(
        shape, lists, state, order[:-1], [pieces[o] for o in order[:-1]],
        fresh=fresh,
    )
    (out,) = attend(
        shape, lists, (q, *state), order[-1:], [pieces[o] for o in order[-1:]],
        last=True,
    )
    return out.reshape(queries.shape)


def solution(mesh):
    mesh_shape = dict(mesh.shape)
    n, cores = mesh_shape["ctx"], mesh_shape["sub"]
    if n & (n - 1) or cores != 2:
        raise ValueError("unsupported mesh")
    split = ("grp", "ctx")
    in_specs = (
        P(split, "kvh", "sub", None),
        P(split, "kvh", None),
        P(split, "kvh", None),
        P(split, "kvh", None),
        P(split, "kvh", None),
        P(split),
        P(split, None),
        P(split, None),
        P(split, None),
    )
    out_specs = P(split, "kvh", "sub", None)
    return jax.shard_map(
        functools.partial(shards, mesh_shape),
        mesh=mesh,
        in_specs=in_specs,
        out_specs=out_specs,
        check_vma=False,
    )
```
